32 devices in a mesh: edata: 4 (over z), expert: 8 (over y, x, core).
Axes of the slice: x: 2, y: 2, z: 4, core: 2. Of those that a mesh axis runs over, the one named last changes fastest.
Arguments:
- tokens: bfloat16 [1024, 4096], P('expert', 'edata'), may hold values from -6 to 6
- grad_out: bfloat16 [1024, 4096], P('expert', 'edata'), may hold values from -6 to 6
- expert_ids: int32 [1024, 8], P('expert'), may hold values from 0 to 15, all different within a row; in each aligned block of 128 rows (0 to 127, 128 to 255, ...) at most 80 rows name the same one
- route_prob: float32 [1024, 8], P('expert'), may hold values from 0.05 to 0.5
- w_gate: bfloat16 [16, 1024, 4096], P('expert', 'edata'), may hold values from -0.09375 to 0.09375
- w_up: bfloat16 [16, 1024, 4096], P('expert', 'edata'), may hold values from -0.09375 to 0.09375
- w_down: bfloat16 [16, 1024, 4096], P('expert', 'edata'), may hold values from -0.1875 to 0.1875
Outputs:
- grad_tokens: bfloat16 [1024, 4096], P('expert', 'edata')
- grad_gate: bfloat16 [16, 1024, 4096], P('expert', 'edata')
- grad_up: bfloat16 [16, 1024, 4096], P('expert', 'edata')
- grad_down: bfloat16 [16, 1024, 4096], P('expert', 'edata')
The draws below stay inside these ranges and needn't reach their ends.
Inputs may be any that keep to these rules, and one draw needn't show every extreme that they name: `expert_ids`: each token names 8 different experts. Among the tokens of one aligned block of 128 no expert is named more than 80 times, and in every draw some expert is named exactly 80 times in some block.
All inputs are finite; a program needn't handle non-finite values.
Results may differ from the reference program's by a relative error of at most 0.012.
Values may be sent and summed in bfloat16 or wider, within the bound.
A program may use at most 192 MiB of HBM per device.

```python
import math
import jax
import jax.numpy as jnp
import numpy as np
from jax import lax

D = 4096
FF = 1024
TOP = 8
TOK_DEV = 128
EXPERTS = 16
TOKENS = 1024
CAP = 80
N_EDATA = 4
N_EXPERT = 8


def block_levels(own_key, extent, split, low, largest):
    loudness, own = 1.0, jax.random.fold_in(own_key, 6)
    for dim, blocks in split:
        heights = jnp.exp(jax.random.uniform(jax.random.fold_in(own, dim), (blocks,), jnp.float32, low / len(split), largest / len(split)))
        loudness = loudness * jnp.repeat(heights, extent[dim] // blocks).reshape([-1 if axis == dim else 1 for axis in range(len(extent))])
    return loudness


def routed_block(key, own, number, rows, count, top, most, skew):
    ranking = jax.random.permutation(key, count)
    packed, common = shares(count, rows * top, most, skew, True), shares(count, rows * top, most, skew, False)
    places = jnp.arange(count)

    def named(tallies, offset_by):
        used = int((tallies > 0).sum())
        fixed = max(1, used // 4)
        shifted = fixed + (places - fixed + offset_by * (used - fixed)) % max(1, count - fixed)
        return jnp.zeros((count,), jnp.int32).at[ranking[jnp.where(places < fixed, places, shifted)]].set(jnp.asarray(tallies, jnp.int32))

    tallies = jnp.where(number % 4 == 0, named(packed, number // 4), named(common, number - number // 4 - 1))
    mixed = jax.random.permutation(jax.random.fold_in(own, 3), count)
    source_of, sink = mixed[0:count // 2 * 2:2], mixed[1:count // 2 * 2:2]
    room = jnp.minimum(tallies[source_of] - 1, most - tallies[sink]) // 2
    room = jnp.where((source_of == ranking[0]) | (sink == ranking[0]) | (tallies[sink] == 0), 0, jnp.maximum(room, 0))
    shifted = jax.random.randint(jax.random.fold_in(own, 4), (count // 2,), 0, 1 << 20) % (room + 1)
    tallies = tallies.at[source_of].add(-shifted).at[sink].add(shifted)
    members = jnp.searchsorted(jnp.cumsum(tallies), jnp.arange(rows * top), side="right").astype(jnp.int32)
    grid = members.reshape(top, rows).T
    grid = grid[jax.random.permutation(jax.random.fold_in(own, 1), rows)]
    offset_by = jax.random.randint(jax.random.fold_in(own, 2), (rows, 1), 0, top)
    return jnp.take_along_axis(grid, (jnp.arange(top)[None, :] + offset_by) % top, axis=1)


def shares(number_of, total, most, skew, full):
    loads = [(1 << 20) // math.isqrt(grade ** skew) + 1 for grade in range(1, number_of + 1)]
    largest = most if full else min(most, max(-(-total // number_of), total * loads[0] // sum(loads)))
    least = 1 if total - largest >= number_of - 1 else 0
    given, rest = [largest] + [least] * (number_of - 1), total - largest - least * (number_of - 1)
    while rest > 0:
        candidates = [i for i in range(1, number_of) if given[i] < largest] or [i for i in range(1, number_of) if given[i] < most]
        pool, left = sum([loads[i] for i in candidates]), rest
        for i in candidates:
            extra = min(most - given[i], max(1, left * loads[i] // pool), rest)
            given[i] = given[i] + extra
            rest = rest - extra
    return np.array(given)


def gaussian(rng, extent, spread, reach, pieces=(), kind=jnp.bfloat16):
    drawn = jax.random.normal(rng, extent, jnp.float32) * spread
    if len(pieces) > 0:
        drawn = block_levels(rng, extent, pieces, -0.22, 0.18) * drawn
    return jnp.clip(drawn, min=-reach, max=reach).astype(kind)


def setup_inputs(seed: int = 0) -> dict:
    key_of = jax.random.split(jax.random.key(seed), 8)
    tokens = gaussian(key_of[0], (TOKENS, D), 1.0, 6.0, ((0, 8), (1, 4)))
    grad_out = gaussian(key_of[1], (TOKENS, D), 1.0, 6.0, ((0, 8), (1, 4)))
    expert_ids_keys = jax.random.split(jax.random.fold_in(key_of[2], 1), TOKENS // TOK_DEV)
    expert_ids_turns = jax.random.permutation(jax.random.fold_in(key_of[2], 3), TOKENS // TOK_DEV)
    expert_ids = jax.vmap(lambda own, number: routed_block(jax.random.fold_in(key_of[2], 2), own, number, TOK_DEV, EXPERTS, TOP, CAP, 1))(expert_ids_keys, expert_ids_turns).reshape((TOKENS, TOP))
    route_prob = jnp.clip(jnp.exp(math.log(0.5) - 2.3025851 * jax.random.uniform(key_of[3], (TOKENS, TOP), jnp.float32) ** block_levels(key_of[3], (TOKENS, TOP), ((0, 8),), -0.2, 0.2)), 0.05, 0.5)
    w_gate = gaussian(key_of[4], (EXPERTS, FF, D), D ** -0.5, 0.09375, ((0, 8), (1, 4)))
    w_up = gaussian(key_of[5], (EXPERTS, FF, D), D ** -0.5, 0.09375, ((0, 8), (1, 4)))
    w_down = gaussian(key_of[6], (EXPERTS, FF, D), FF ** -0.5, 0.1875, ((0, 8), (1, 4)))
    return dict(tokens=tokens, grad_out=grad_out, expert_ids=expert_ids, route_prob=route_prob, w_gate=w_gate, w_up=w_up, w_down=w_down)


def reference(tokens, grad_out, expert_ids, route_prob, w_gate, w_up, w_down):
    pair_count = TOK_DEV * TOP
    blocks = expert_ids.reshape(N_EXPERT, pair_count)
    onehot = (blocks[:, :, None] == jnp.arange(EXPERTS, dtype=jnp.int32)[None, None, :]).astype(jnp.int32)
    slots = jnp.sum((jnp.cumsum(onehot, 1) - onehot) * onehot, 2).astype(jnp.int32)
    source = jnp.broadcast_to(jnp.arange(N_EXPERT, dtype=jnp.int32)[:, None], (N_EXPERT, pair_count))
    global_pair = source * pair_count + jnp.arange(pair_count, dtype=jnp.int32)[None, :]
    table = jnp.full((EXPERTS, N_EXPERT, CAP), TOKENS * TOP, jnp.int32)
    table = table.at[blocks, source, slots].set(global_pair)
    x_padded = jnp.concatenate([tokens, jnp.zeros((1, D), jnp.bfloat16)], 0)
    dy_padded = jnp.concatenate([grad_out, jnp.zeros((1, D), jnp.bfloat16)], 0)
    prob_padded = jnp.concatenate([route_prob.reshape(-1), jnp.zeros((1,), jnp.float32)], 0)
    group = FF // N_EDATA

    def one_expert(carry, inputs):
        rows, weight_gate, weight_up, weight_down = inputs
        rows = rows.reshape(-1)
        token_of = (rows // TOP).astype(jnp.int32)
        xs = x_padded[token_of]
        ds = (prob_padded[rows][:, None] * dy_padded[token_of].astype(jnp.float32)).astype(jnp.bfloat16)
        gate_value = jnp.dot(xs, weight_gate.T, preferred_element_type=jnp.float32)
        up_value = jnp.dot(xs, weight_up.T, preferred_element_type=jnp.float32)
        sigma = jax.nn.sigmoid(gate_value)
        active = gate_value * sigma
        hidden = (active * up_value).astype(jnp.bfloat16)
        back = jnp.dot(ds, weight_down.T, preferred_element_type=jnp.float32)
        gate_grad = (back * up_value * sigma * (1.0 + gate_value * (1.0 - sigma))).astype(jnp.bfloat16)
        up_grad = (back * active).astype(jnp.bfloat16)
        grad_g = jnp.dot(gate_grad.T, xs, preferred_element_type=jnp.float32).astype(jnp.bfloat16)
        grad_u = jnp.dot(up_grad.T, xs, preferred_element_type=jnp.float32).astype(jnp.bfloat16)
        grad_d = jnp.dot(hidden.T, ds, preferred_element_type=jnp.float32).astype(jnp.bfloat16)
        total = jnp.zeros((rows.shape[0], D), jnp.float32)
        for index in range(N_EDATA):
            lower = index * group
            upper = lower + group
            part = jnp.dot(gate_grad[:, lower:upper], weight_gate[lower:upper, :], preferred_element_type=jnp.float32)
            part = part + jnp.dot(up_grad[:, lower:upper], weight_up[lower:upper, :], preferred_element_type=jnp.float32)
            part = lax.optimization_barrier(part.astype(jnp.bfloat16))
            total = total + part.astype(jnp.float32)
        carry = carry.at[token_of].add(total)
        return carry, (grad_g, grad_u, grad_d)

    start = jnp.zeros((TOKENS + 1, D), jnp.float32)
    final, grads = lax.scan(one_expert, start, (table, w_gate, w_up, w_down))
    grad_tokens = final[:TOKENS].astype(jnp.bfloat16)
    return (grad_tokens, grads[0], grads[1], grads[2])
```

```python
import jax
import jax.numpy as jnp
from jax import lax
from jax.sharding import PartitionSpec as P


def block_senders(ids, experts_all, capacity):
    token_count, top_count = ids.shape
    pair_count = token_count * top_count
    flat_ids = ids.reshape(pair_count)
    onehot = (flat_ids[:, None] == jnp.arange(experts_all, dtype=jnp.int32)[None, :]).astype(
        jnp.int32
    )
    earlier = jnp.cumsum(onehot, 0) - onehot
    slots = jnp.sum(earlier * onehot, 1)
    target = flat_ids * capacity + slots
    sender = jnp.full((experts_all * capacity,), pair_count, jnp.int32)
    sender = sender.at[target].set(jnp.arange(pair_count, dtype=jnp.int32))
    return target, sender


def body(tokens, grad_out, expert_ids, route_prob, w_gate, w_up, w_down):
    token_count, top_count = expert_ids.shape
    local_experts = w_gate.shape[0]
    expert_devices = lax.axis_size("expert")
    me = lax.axis_index("expert")
    experts_all = expert_devices * local_experts
    capacity = token_count * top_count * 5 // (4 * experts_all)
    pair_count = token_count * top_count
    target, _ = block_senders(expert_ids, experts_all, capacity)
    all_ids = lax.all_gather(expert_ids, "expert", axis=0, tiled=False)
    all_prob = lax.all_gather(route_prob, "expert", axis=0, tiled=False)
    _, senders = jax.vmap(lambda i: block_senders(i, experts_all, capacity))(all_ids)
    mine = lax.dynamic_slice_in_dim(senders, me * local_experts * capacity, local_experts * capacity, 1)
    valid = mine < pair_count
    source = jnp.arange(expert_devices, dtype=jnp.int32)[:, None]
    total_tokens = expert_devices * token_count
    token_of = jnp.where(valid, source * token_count + mine // top_count, total_tokens).reshape(-1)
    flat_prob = jnp.concatenate(
        [all_prob.reshape(expert_devices, pair_count), jnp.zeros((expert_devices, 1), jnp.float32)], 1
    )
    prob_of = jnp.take_along_axis(flat_prob, jnp.minimum(mine, pair_count), 1).reshape(-1)
    whole_x = lax.all_gather(tokens, "edata", axis=1, tiled=True)
    whole_dy = lax.all_gather(grad_out, "edata", axis=1, tiled=True)
    all_x = lax.all_gather(whole_x, "expert", axis=0, tiled=True)
    all_dy = lax.all_gather(whole_dy, "expert", axis=0, tiled=True)
    width = all_x.shape[1]
    padded_x = jnp.concatenate([all_x, jnp.zeros((1, width), jnp.bfloat16)], 0)
    padded_dy = jnp.concatenate([all_dy, jnp.zeros((1, width), jnp.bfloat16)], 0)
    slot_x = padded_x[token_of].reshape(expert_devices, local_experts, capacity, width)
    slot_dy = (prob_of[:, None] * padded_dy[token_of].astype(jnp.float32)).astype(jnp.bfloat16)
    slot_dy = slot_dy.reshape(expert_devices, local_experts, capacity, width)
    gate_value = jnp.einsum("sxcd,xfd->sxcf", slot_x, w_gate, preferred_element_type=jnp.float32)
    up_value = jnp.einsum("sxcd,xfd->sxcf", slot_x, w_up, preferred_element_type=jnp.float32)
    sigma = jax.nn.sigmoid(gate_value)
    active = gate_value * sigma
    hidden = (active * up_value).astype(jnp.bfloat16)
    back = jnp.einsum("sxcd,xfd->sxcf", slot_dy, w_down, preferred_element_type=jnp.float32)
    gate_grad = (back * up_value * sigma * (1.0 + gate_value * (1.0 - sigma))).astype(jnp.bfloat16)
    up_grad = (back * active).astype(jnp.bfloat16)
    grad_gate = jnp.einsum(
        "sxcf,sxcd->xfd", gate_grad, slot_x, preferred_element_type=jnp.float32
    ).astype(jnp.bfloat16)
    grad_up = jnp.einsum(
        "sxcf,sxcd->xfd", up_grad, slot_x, preferred_element_type=jnp.float32
    ).astype(jnp.bfloat16)
    grad_down = jnp.einsum(
        "sxcf,sxcd->xfd", hidden, slot_dy, preferred_element_type=jnp.float32
    ).astype(jnp.bfloat16)
    partial_value = jnp.einsum(
        "sxcf,xfd->sxcd", gate_grad, w_gate, preferred_element_type=jnp.float32
    )
    partial_value = partial_value + jnp.einsum(
        "sxcf,xfd->sxcd", up_grad, w_up, preferred_element_type=jnp.float32
    )
    partial_value = partial_value.astype(jnp.bfloat16)
    returned = lax.all_to_all(
        partial_value.reshape(expert_devices, local_experts * capacity, -1),
        "expert",
        split_axis=0,
        concat_axis=0,
        tiled=True,
    )
    width = returned.shape[-1]
    picked = returned.reshape(experts_all * capacity, width)[target]
    per_token = jnp.sum(picked.reshape(token_count, top_count, width), 1, dtype=jnp.float32)
    grad_tokens = lax.psum_scatter(per_token, "edata", scatter_dimension=1, tiled=True).astype(
        jnp.bfloat16
    )
    return (grad_tokens, grad_gate, grad_up, grad_down)


def solution(mesh):
    placed = (
        P("expert", "edata"),
        P("expert", "edata"),
        P("expert", None),
        P("expert", None),
        P("expert", "edata", None),
        P("expert", "edata", None),
        P("expert", "edata", None),
    )
    return jax.shard_map(
        body,
        mesh=mesh,
        in_specs=placed,
        out_specs=(
            P("expert", "edata"),
            P("expert", "edata", None),
            P("expert", "edata", None),
            P("expert", "edata", None),
        ),
        check_vma=False,
    )
```

```python
import jax
import jax.numpy as jnp
from jax import lax
from jax.sharding import PartitionSpec as P


def ranks(onehot):
    pair_count = onehot.shape[-2]
    row = lax.broadcasted_iota(jnp.int32, (pair_count, pair_count), 0)
    col = lax.broadcasted_iota(jnp.int32, (pair_count, pair_count), 1)
    tri = (col < row).astype(jnp.bfloat16)
    earlier = jnp.einsum(
        "pq,...qe->...pe", tri, onehot.astype(jnp.bfloat16), preferred_element_type=jnp.float32
    )
    return earlier.astype(jnp.int32)


def body(tokens, grad_out, expert_ids, route_prob, w_gate, w_up, w_down):
    token_count, top_count = expert_ids.shape
    local_experts = w_gate.shape[0]
    expert_devices = lax.axis_size("expert")
    me = lax.axis_index("expert")
    experts_all = expert_devices * local_experts
    capacity = token_count * top_count * 5 // (4 * experts_all)
    pair_count = token_count * top_count
    cap_iota = jnp.arange(capacity, dtype=jnp.int32)

    all_ids = lax.all_gather(expert_ids, "expert", axis=0, tiled=False)
    all_prob = lax.all_gather(route_prob, "expert", axis=0, tiled=False)
    mine = me * local_experts + jnp.arange(local_experts, dtype=jnp.int32)
    named = all_ids.reshape(expert_devices, pair_count)[:, :, None] == mine
    rank = ranks(named)
    hit = named[..., None] & (rank[..., None] == cap_iota)
    hit = hit.reshape(expert_devices, token_count, top_count, local_experts, capacity)
    pick = jnp.sum(hit.astype(jnp.int32), 2).astype(jnp.bfloat16)
    prob_of = jnp.sum(jnp.where(hit, all_prob[:, :, :, None, None], 0.0), (1, 2))

    whole_x = lax.all_gather(tokens, "edata", axis=1, tiled=True)
    whole_dy = lax.all_gather(grad_out, "edata", axis=1, tiled=True)
    all_x = lax.all_gather(whole_x, "expert", axis=0, tiled=False)
    all_dy = lax.all_gather(whole_dy, "expert", axis=0, tiled=False)
    slot_x = jnp.einsum(
        "stxc,std->sxcd", pick, all_x, preferred_element_type=jnp.float32
    ).astype(jnp.bfloat16)
    slot_dy = jnp.einsum("stxc,std->sxcd", pick, all_dy, preferred_element_type=jnp.float32)
    slot_dy = (prob_of[..., None] * slot_dy).astype(jnp.bfloat16)

    gate_value = jnp.einsum("sxcd,xfd->sxcf", slot_x, w_gate, preferred_element_type=jnp.float32)
    up_value = jnp.einsum("sxcd,xfd->sxcf", slot_x, w_up, preferred_element_type=jnp.float32)
    sigma = jax.nn.sigmoid(gate_value)
    active = gate_value * sigma
    hidden = (active * up_value).astype(jnp.bfloat16)
    back = jnp.einsum("sxcd,xfd->sxcf", slot_dy, w_down, preferred_element_type=jnp.float32)
    gate_grad = (back * up_value * sigma * (1.0 + gate_value * (1.0 - sigma))).astype(jnp.bfloat16)
    up_grad = (back * active).astype(jnp.bfloat16)
    grad_gate = jnp.einsum(
        "sxcf,sxcd->xfd", gate_grad, slot_x, preferred_element_type=jnp.float32
    ).astype(jnp.bfloat16)
    grad_up = jnp.einsum(
        "sxcf,sxcd->xfd", up_grad, slot_x, preferred_element_type=jnp.float32
    ).astype(jnp.bfloat16)
    grad_down = jnp.einsum(
        "sxcf,sxcd->xfd", hidden, slot_dy, preferred_element_type=jnp.float32
    ).astype(jnp.bfloat16)
    partial_value = jnp.einsum(
        "sxcf,xfd->sxcd", gate_grad, w_gate, preferred_element_type=jnp.float32
    )
    partial_value = partial_value + jnp.einsum(
        "sxcf,xfd->sxcd", up_grad, w_up, preferred_element_type=jnp.float32
    )
    partial_value = partial_value.astype(jnp.bfloat16)
    returned = lax.all_to_all(
        partial_value.reshape(expert_devices, local_experts * capacity, -1),
        "expert",
        split_axis=0,
        concat_axis=0,
        tiled=True,
    )
    width = returned.shape[-1]

    own = expert_ids.reshape(pair_count, 1) == jnp.arange(experts_all, dtype=jnp.int32)
    slot = jnp.sum(jnp.where(own, ranks(own), 0), 1)
    back_hit = own[:, :, None] & (slot[:, None, None] == cap_iota)
    gather_back = jnp.sum(
        back_hit.reshape(token_count, top_count, experts_all * capacity).astype(jnp.int32), 1
    ).astype(jnp.bfloat16)
    per_token = jnp.einsum(
        "tq,qd->td",
        gather_back,
        returned.reshape(experts_all * capacity, width),
        preferred_element_type=jnp.float32,
    )
    grad_tokens = lax.psum_scatter(per_token, "edata", scatter_dimension=1, tiled=True).astype(
        jnp.bfloat16
    )
    return (grad_tokens, grad_gate, grad_up, grad_down)


def solution(mesh):
    placed = (
        P("expert", "edata"),
        P("expert", "edata"),
        P("expert", None),
        P("expert", None),
        P("expert", "edata", None),
        P("expert", "edata", None),
        P("expert", "edata", None),
    )
    return jax.shard_map(
        body,
        mesh=mesh,
        in_specs=placed,
        out_specs=(
            P("expert", "edata"),
            P("expert", "edata", None),
            P("expert", "edata", None),
            P("expert", "edata", None),
        ),
        check_vma=False,
    )
```

```python
import jax
import jax.numpy as jnp
from jax import lax
from jax.sharding import PartitionSpec as P


def ranks(onehot):
    pair_count = onehot.shape[-2]
    row = lax.broadcasted_iota(jnp.int32, (pair_count, pair_count), 0)
    col = lax.broadcasted_iota(jnp.int32, (pair_count, pair_count), 1)
    tri = (col < row).astype(jnp.bfloat16)
    earlier = jnp.einsum(
        "pq,...qe->...pe", tri, onehot.astype(jnp.bfloat16), preferred_element_type=jnp.float32
    )
    return earlier.astype(jnp.int32)


def body(tokens, grad_out, expert_ids, route_prob, w_gate, w_up, w_down):
    token_count, top_count = expert_ids.shape
    local_experts = w_gate.shape[0]
    expert_devices = lax.axis_size("expert")
    me = lax.axis_index("expert")
    experts_all = expert_devices * local_experts
    capacity = token_count * top_count * 5 // (4 * experts_all)
    pair_count = token_count * top_count
    cap_iota = jnp.arange(capacity, dtype=jnp.int32)

    all_ids = lax.all_gather(expert_ids, "expert", axis=0, tiled=False)
    all_prob = lax.all_gather(route_prob, "expert", axis=0, tiled=False)
    mine = me * local_experts + jnp.arange(local_experts, dtype=jnp.int32)
    named = all_ids.reshape(expert_devices, pair_count)[:, :, None] == mine
    rank = ranks(named)
    hit = named[..., None] & (rank[..., None] == cap_iota)
    hit = hit.reshape(expert_devices, token_count, top_count, local_experts, capacity)
    pick = jnp.sum(hit.astype(jnp.int32), 2).astype(jnp.bfloat16)
    prob_of = jnp.sum(jnp.where(hit, all_prob[:, :, :, None, None], 0.0), (1, 2))

    both = lax.all_gather(jnp.stack([tokens, grad_out]), "edata", axis=2, tiled=True)
    both = lax.all_gather(both, "expert", axis=1, tiled=False)
    all_x, all_dy = both[0], both[1]
    slot_x = jnp.einsum(
        "stxc,std->sxcd", pick, all_x, preferred_element_type=jnp.float32
    ).astype(jnp.bfloat16)
    slot_dy = jnp.einsum("stxc,std->sxcd", pick, all_dy, preferred_element_type=jnp.float32)
    slot_dy = (prob_of[..., None] * slot_dy).astype(jnp.bfloat16)

    gate_value = jnp.einsum("sxcd,xfd->sxcf", slot_x, w_gate, preferred_element_type=jnp.float32)
    up_value = jnp.einsum("sxcd,xfd->sxcf", slot_x, w_up, preferred_element_type=jnp.float32)
    sigma = jax.nn.sigmoid(gate_value)
    active = gate_value * sigma
    hidden = (active * up_value).astype(jnp.bfloat16)
    back = jnp.einsum("sxcd,xfd->sxcf", slot_dy, w_down, preferred_element_type=jnp.float32)
    gate_grad = (back * up_value * sigma * (1.0 + gate_value * (1.0 - sigma))).astype(jnp.bfloat16)
    up_grad = (back * active).astype(jnp.bfloat16)
    grad_gate = jnp.einsum(
        "sxcf,sxcd->xfd", gate_grad, slot_x, preferred_element_type=jnp.float32
    ).astype(jnp.bfloat16)
    grad_up = jnp.einsum(
        "sxcf,sxcd->xfd", up_grad, slot_x, preferred_element_type=jnp.float32
    ).astype(jnp.bfloat16)
    grad_down = jnp.einsum(
        "sxcf,sxcd->xfd", hidden, slot_dy, preferred_element_type=jnp.float32
    ).astype(jnp.bfloat16)
    partial_value = jnp.einsum(
        "sxcf,xfd->sxcd", gate_grad, w_gate, preferred_element_type=jnp.float32
    )
    partial_value = partial_value + jnp.einsum(
        "sxcf,xfd->sxcd", up_grad, w_up, preferred_element_type=jnp.float32
    )
    partial_value = partial_value.astype(jnp.bfloat16)
    returned = lax.all_to_all(
        partial_value.reshape(expert_devices, local_experts * capacity, -1),
        "expert",
        split_axis=0,
        concat_axis=0,
        tiled=True,
    )
    width = returned.shape[-1]

    own = expert_ids.reshape(pair_count, 1) == jnp.arange(experts_all, dtype=jnp.int32)
    slot = jnp.sum(jnp.where(own, ranks(own), 0), 1)
    back_hit = own[:, :, None] & (slot[:, None, None] == cap_iota)
    gather_back = jnp.sum(
        back_hit.reshape(token_count, top_count, experts_all * capacity).astype(jnp.int32), 1
    ).astype(jnp.bfloat16)
    per_token = jnp.einsum(
        "tq,qd->td",
        gather_back,
        returned.reshape(experts_all * capacity, width),
        preferred_element_type=jnp.float32,
    )
    grad_tokens = lax.psum_scatter(per_token, "edata", scatter_dimension=1, tiled=True).astype(
        jnp.bfloat16
    )
    return (grad_tokens, grad_gate, grad_up, grad_down)


def solution(mesh):
    placed = (
        P("expert", "edata"),
        P("expert", "edata"),
        P("expert", None),
        P("expert", None),
        P("expert", "edata", None),
        P("expert", "edata", None),
        P("expert", "edata", None),
    )
    return jax.shard_map(
        body,
        mesh=mesh,
        in_specs=placed,
        out_specs=(
            P("expert", "edata"),
            P("expert", "edata", None),
            P("expert", "edata", None),
            P("expert", "edata", None),
        ),
        check_vma=False,
    )
```

```python
import jax
import jax.numpy as jnp
from jax import lax
from jax.sharding import PartitionSpec as P


def ranks(onehot):
    pair_count = onehot.shape[-2]
    row = lax.broadcasted_iota(jnp.int32, (pair_count, pair_count), 0)
    col = lax.broadcasted_iota(jnp.int32, (pair_count, pair_count), 1)
    tri = (col < row).astype(jnp.bfloat16)
    earlier = jnp.einsum(
        "pq,...qe->...pe", tri, onehot.astype(jnp.bfloat16), preferred_element_type=jnp.float32
    )
    return earlier.astype(jnp.int32)


def body(tokens, grad_out, expert_ids, route_prob, w_gate, w_up, w_down):
    token_count, top_count = expert_ids.shape
    local_experts = w_gate.shape[0]
    expert_devices = lax.axis_size("expert")
    me = lax.axis_index("expert")
    experts_all = expert_devices * local_experts
    capacity = token_count * top_count * 5 // (4 * experts_all)
    pair_count = token_count * top_count
    cap_iota = jnp.arange(capacity, dtype=jnp.int32)

    routing = jnp.stack([expert_ids.astype(jnp.float32), route_prob])
    routing = lax.all_gather(routing, "expert", axis=1, tiled=False)
    all_ids, all_prob = routing[0].astype(jnp.int32), routing[1]
    mine = me * local_experts + jnp.arange(local_experts, dtype=jnp.int32)
    named = all_ids.reshape(expert_devices, pair_count)[:, :, None] == mine
    rank = ranks(named)
    hit = named[..., None] & (rank[..., None] == cap_iota)
    hit = hit.reshape(expert_devices, token_count, top_count, local_experts, capacity)
    pick = jnp.sum(hit.astype(jnp.int32), 2).astype(jnp.bfloat16)
    prob_of = jnp.sum(jnp.where(hit, all_prob[:, :, :, None, None], 0.0), (1, 2))

    both = lax.all_gather(jnp.stack([tokens, grad_out]), "edata", axis=2, tiled=True)
    both = lax.all_gather(both, "expert", axis=1, tiled=False)
    all_x, all_dy = both[0], both[1]
    slot_x = jnp.einsum(
        "stxc,std->sxcd", pick, all_x, preferred_element_type=jnp.float32
    ).astype(jnp.bfloat16)
    slot_dy = jnp.einsum("stxc,std->sxcd", pick, all_dy, preferred_element_type=jnp.float32)
    slot_dy = (prob_of[..., None] * slot_dy).astype(jnp.bfloat16)

    gate_value = jnp.einsum("sxcd,xfd->sxcf", slot_x, w_gate, preferred_element_type=jnp.float32)
    up_value = jnp.einsum("sxcd,xfd->sxcf", slot_x, w_up, preferred_element_type=jnp.float32)
    sigma = jax.nn.sigmoid(gate_value)
    active = gate_value * sigma
    hidden = (active * up_value).astype(jnp.bfloat16)
    back = jnp.einsum("sxcd,xfd->sxcf", slot_dy, w_down, preferred_element_type=jnp.float32)
    gate_grad = (back * up_value * sigma * (1.0 + gate_value * (1.0 - sigma))).astype(jnp.bfloat16)
    up_grad = (back * active).astype(jnp.bfloat16)
    grad_gate = jnp.einsum(
        "sxcf,sxcd->xfd", gate_grad, slot_x, preferred_element_type=jnp.float32
    ).astype(jnp.bfloat16)
    grad_up = jnp.einsum(
        "sxcf,sxcd->xfd", up_grad, slot_x, preferred_element_type=jnp.float32
    ).astype(jnp.bfloat16)
    grad_down = jnp.einsum(
        "sxcf,sxcd->xfd", hidden, slot_dy, preferred_element_type=jnp.float32
    ).astype(jnp.bfloat16)
    partial_value = jnp.einsum(
        "sxcf,xfd->sxcd", gate_grad, w_gate, preferred_element_type=jnp.float32
    )
    partial_value = partial_value + jnp.einsum(
        "sxcf,xfd->sxcd", up_grad, w_up, preferred_element_type=jnp.float32
    )
    partial_value = partial_value.astype(jnp.bfloat16)
    returned = lax.all_to_all(
        partial_value.reshape(expert_devices, local_experts * capacity, -1),
        "expert",
        split_axis=0,
        concat_axis=0,
        tiled=True,
    )
    width = returned.shape[-1]

    own = expert_ids.reshape(pair_count, 1) == jnp.arange(experts_all, dtype=jnp.int32)
    slot = jnp.sum(jnp.where(own, ranks(own), 0), 1)
    back_hit = own[:, :, None] & (slot[:, None, None] == cap_iota)
    gather_back = jnp.sum(
        back_hit.reshape(token_count, top_count, experts_all * capacity).astype(jnp.int32), 1
    ).astype(jnp.bfloat16)
    per_token = jnp.einsum(
        "tq,qd->td",
        gather_back,
        returned.reshape(experts_all * capacity, width),
        preferred_element_type=jnp.float32,
    )
    grad_tokens = lax.psum_scatter(per_token, "edata", scatter_dimension=1, tiled=True).astype(
        jnp.bfloat16
    )
    return (grad_tokens, grad_gate, grad_up, grad_down)


def solution(mesh):
    placed = (
        P("expert", "edata"),
        P("expert", "edata"),
        P("expert", None),
        P("expert", None),
        P("expert", "edata", None),
        P("expert", "edata", None),
        P("expert", "edata", None),
    )
    return jax.shard_map(
        body,
        mesh=mesh,
        in_specs=placed,
        out_specs=(
            P("expert", "edata"),
            P("expert", "edata", None),
            P("expert", "edata", None),
            P("expert", "edata", None),
        ),
        check_vma=False,
    )
```
